32 devices in a mesh: groups: 2 (over y), mom: 4 (over z), lat: 2 (over x), band: 2 (over core).
Axes of the slice: x: 2, y: 2, z: 4, core: 2. Of those that a mesh axis runs over, the one named last changes fastest.
Arguments:
- table: bfloat16 [2048, 2, 32, 32], P(('groups', 'mom', 'lat'), None, None, 'band'), parts along dimension 0, may hold values from -0.1875 to 0.1875
- lattice: int32 [1024, 6], P(('mom', 'lat')), may hold values from -6 to 6
- pairs: int32 [6, 4096], P(None, ('groups', 'mom')), parts along dimension 1, may hold values from 0 to 23
- left_rot: float32 [4096, 2, 32, 32], P(('groups', 'mom', 'lat')), parts along dimension 0, may hold values from -0.75 to 0.75
- right_rotation: float32 [4096, 2, 32, 32], P(('groups', 'mom', 'lat'), None, 'band'), parts along dimension 0, may hold values from -0.75 to 0.75
Outputs:
- coupling: float32 [4096, 2, 32, 32], P(('groups', 'mom', 'lat'), None, None, 'band'), parts along dimension 0
The draws below stay inside these ranges and needn't reach their ends.
There are 2 independent parts, one for each index of `groups`. The reference program is written for one: setup_inputs(seed, part) draws one part's arguments, and reference() takes and returns one part's arrays. A program takes and returns all parts, laid end to end along the dimension named above; an argument that names none is the same for every part. Nothing has to cross between parts.
All inputs are finite; a program needn't handle non-finite values.
Results may differ from the reference program's by a relative error of at most 0.0018.
Values may be sent and summed in bfloat16 or wider, within the bound.
A program may use at most 128 MiB of HBM per device.

```python
import math
import jax
import jax.numpy as jnp
from jax import lax

NB = 32
NK = 24
LMAX = 6
NP = 2048
NR = 1024


def plant(result, rng, least, high):
    longest = result.shape.index(max(result.shape))
    spots = []
    for shift in (0, 1):
        where = [jax.random.randint(jax.random.fold_in(rng, axis), (), 0, length) for axis, length in enumerate(result.shape)]
        where[longest] = (where[longest] + shift) % result.shape[longest]
        spots.append(tuple(where))
    return result.at[spots[0]].set(least).at[spots[1]].set(high)


def block_levels(key, dims, pieces, least, high):
    def one(axis_at, shards_of):
        steps = jax.random.uniform(jax.random.fold_in(jax.random.fold_in(key, 6), axis_at), (shards_of,), jnp.float32, least / len(pieces), high / len(pieces))
        return jnp.repeat(jnp.exp(steps), dims[axis_at] // shards_of).reshape((-1,) + (1,) * (len(dims) - axis_at - 1))

    factor_of = one(*pieces[0])
    for cut in pieces[1:]:
        factor_of = factor_of * one(*cut)
    return factor_of


def scatter_about(own_key, dims, spread, bound, pieces=(), dtype=jnp.bfloat16):
    array = jax.random.normal(own_key, dims, jnp.float32) * spread
    if len(pieces) > 0:
        array = block_levels(own_key, dims, pieces, -0.22, 0.18) * array
    return jnp.clip(array, min=-bound, max=bound).astype(dtype)


def setup_inputs(seed: int = 0, part: int = 0) -> dict:
    arg_keys = jax.random.split(jax.random.key(seed), 6)
    part_keys = jax.random.split(jax.random.fold_in(arg_keys[5], part), 6)
    return {
        "table": scatter_about(part_keys[0], (NR, 2, NB, NB), NR ** -0.5, 0.1875, ((0, 8), (3, 2))),
        "lattice": plant(jax.random.randint(arg_keys[1], (NR, 6), 0 - LMAX, LMAX + 1), jax.random.fold_in(arg_keys[1], 1), 0 - LMAX, LMAX).astype(jnp.int32),
        "pairs": plant(jax.random.randint(part_keys[2], (6, NP), 0, NK), jax.random.fold_in(part_keys[2], 1), 0, NK - 1).astype(jnp.int32),
        "left_rot": scatter_about(part_keys[3], (NP, 2, NB, NB), (2 * NB) ** -0.5, 0.75, ((0, 8),), jnp.float32),
        "right_rotation": scatter_about(part_keys[4], (NP, 2, NB, NB), (2 * NB) ** -0.5, 0.75, ((0, 8), (2, 2)), jnp.float32),
    }


def bloch_block(kq, lattice, flat):
    turn = kq[:, 0][:, None] * lattice[:, 0][None, :]
    for comp in range(1, 6):
        turn = turn + kq[:, comp][:, None] * lattice[:, comp][None, :]
    turn = jnp.mod(turn, NK)
    angle = turn.astype(jnp.float32) * jnp.float32(2.0 * math.pi / NK)
    cosine = jnp.cos(angle).astype(jnp.bfloat16)
    sine = jnp.sin(angle).astype(jnp.bfloat16)
    cos_part = jnp.dot(cosine, flat, preferred_element_type=jnp.float32)
    sin_part = jnp.dot(sine, flat, preferred_element_type=jnp.float32)
    half = NB * NB
    real_part = cos_part[:, :half] - sin_part[:, half:]
    imag_part = cos_part[:, half:] + sin_part[:, :half]
    return real_part, imag_part


def reference(table, lattice, pairs, left_rot, right_rotation):
    flat = table.reshape(NR, 2 * NB * NB)
    block = math.gcd(NP, 512)
    count = NP // block
    grouped = pairs.T.reshape(count, block, 6)
    real_part, imag_part = lax.map(lambda kq: bloch_block(kq, lattice, flat), grouped)
    bre = real_part.reshape(NP, NB, NB)
    bim = imag_part.reshape(NP, NB, NB)
    upper_bound = lax.Precision.HIGHEST
    ure = left_rot[:, 0].astype(jnp.float32)
    uim = left_rot[:, 1].astype(jnp.float32)
    left_real = jnp.einsum('pmk,pmn->pkn', ure, bre, precision=upper_bound) + jnp.einsum('pmk,pmn->pkn', uim, bim, precision=upper_bound)
    left_imaginary = jnp.einsum('pmk,pmn->pkn', ure, bim, precision=upper_bound) - jnp.einsum('pmk,pmn->pkn', uim, bre, precision=upper_bound)
    vector_real = right_rotation[:, 0].astype(jnp.float32)
    vector_imaginary = right_rotation[:, 1].astype(jnp.float32)
    coupling_real = jnp.einsum('hsq,hqi->hsi', left_real, vector_real, precision=upper_bound) - jnp.einsum('hsq,hqi->hsi', left_imaginary, vector_imaginary, precision=upper_bound)
    coupling_imaginary = jnp.einsum('hsq,hqi->hsi', left_real, vector_imaginary, precision=upper_bound) + jnp.einsum('hsq,hqi->hsi', left_imaginary, vector_real, precision=upper_bound)
    return jnp.stack([coupling_real, coupling_imaginary], axis=1)
```

```python
import functools
import math

import jax
import jax.numpy as jnp
import numpy as np
from jax import lax
from jax.experimental import pallas as pl
from jax.experimental.pallas import tpu as pltpu
from jax.sharding import PartitionSpec as P

NK = 24
F32 = jnp.float32
BF16 = jnp.bfloat16


def _sine_fit():
    b = 6.0 * np.sin(np.linspace(1e-3, math.pi / 2, 400))
    cols = np.stack([b ** (2 * j + 1) for j in range(5)], 1)
    scale = np.abs(cols).max(0)
    sol = np.linalg.lstsq(cols / scale, np.sin(math.pi * b / 12), rcond=None)[0]
    return [float(np.float32(v)) for v in sol / scale]


SINE = _sine_fit()


def quarter_sine(b):
    x = b * b
    acc = x * SINE[4] + SINE[3]
    acc = acc * x + SINE[2]
    acc = acc * x + SINE[1]
    acc = acc * x + SINE[0]
    return acc * b


def loop(count, body):
    if count <= 4:
        for i in range(count):
            body(i)
    else:
        def step(i, carry):
            body(i)
            return carry
        lax.fori_loop(0, count, step, 0)


def kernel(
    cfg, table, lattice, pairs, left, right, out,
    gath, lats, phase_a, phase_b, bloch, lbuf, rbuf, rother, tmine, tother,
    lat_send, lat_recv, tab_send, tab_recv, own_sem, in_sem, swap_send, swap_recv,
):
    moms, lat_n, chunks, mc, nb_loc, owned, bands = cfg
    shards = moms * lat_n
    z = lax.axis_index("mom")
    x = lax.axis_index("lat")
    core = lax.axis_index("band")
    me = z * lat_n + x
    other = 1 - core
    rloc = table.shape[3]
    lane_tiles = owned // 128

    lcopy = pltpu.make_async_copy(left, lbuf, in_sem.at[0])
    rcopy = pltpu.make_async_copy(right, rbuf, in_sem.at[1])
    lcopy.start()
    rcopy.start()

    barrier = pltpu.get_barrier_semaphore()

    def greet(q, carry):
        @pl.when(q != me)
        def _():
            pl.semaphore_signal(
                barrier, inc=1,
                device_id={"mom": q // lat_n, "lat": q % lat_n},
                device_id_type=pl.DeviceIdType.MESH,
            )
        return carry

    lax.fori_loop(0, shards, greet, 0)
    pl.semaphore_signal(
        barrier, inc=1, device_id={"band": other},
        device_id_type=pl.DeviceIdType.MESH,
    )
    pl.semaphore_wait(barrier, shards)

    def lat_copy(q, slot, sem_at):
        return pltpu.make_async_remote_copy(
            src_ref=lattice, dst_ref=lats.at[slot],
            send_sem=lat_send.at[sem_at], recv_sem=lat_recv.at[slot],
            device_id={"mom": q // lat_n, "lat": q % lat_n},
            device_id_type=pl.DeviceIdType.MESH,
        )

    def lat_out(q, carry):
        @pl.when(q != me)
        def _():
            lat_copy(q, me, q).start()
        return carry

    lax.fori_loop(0, shards, lat_out, 0)
    lat_own = pltpu.make_async_copy(lattice, lats.at[me], own_sem.at[chunks])
    lat_own.start()

    def tab_copy(src, slot, c, way):
        step = 1 if way % 2 == 0 else -1
        dev = {"mom": z + step} if way < 2 else {"lat": x + step}
        return pltpu.make_async_remote_copy(
            src_ref=src, dst_ref=gath.at[c, slot],
            send_sem=tab_send.at[way, slot, c], recv_sem=tab_recv.at[slot, c],
            device_id=dev, device_id_type=pl.DeviceIdType.MESH,
        )

    def sent_ways(slot):
        j = slot // lat_n
        i = slot % lat_n
        return (
            (i == x) & (j <= z) & (z < moms - 1),
            (i == x) & (j >= z) & (z > 0),
            (i <= x) & (x < lat_n - 1),
            (i >= x) & (x > 0),
        )

    def pass_on(src, slot, c, ways=(0, 1, 2, 3)):
        conds = sent_ways(slot)
        for way in ways:
            @pl.when(conds[way])
            def _(way=way):
                tab_copy(src, slot, c, way).start()

    for c in range(chunks):
        pass_on(table.at[:, pl.ds(c * mc, mc)], me, c)
    own = [
        pltpu.make_async_copy(
            table.at[:, pl.ds(c * mc, mc)], gath.at[c, me], own_sem.at[c]
        )
        for c in range(chunks)
    ]
    for c in range(chunks):
        own[c].start()

    half = nb_loc
    rcopy.wait()
    rswap = pltpu.make_async_remote_copy(
        src_ref=rbuf.at[:, :, pl.ds(pl.multiple_of(other * half, 8), half)],
        dst_ref=rother, send_sem=swap_send.at[0], recv_sem=swap_recv.at[0],
        device_id={"band": other}, device_id_type=pl.DeviceIdType.MESH,
    )
    rswap.start()

    lat_own.wait()
    kq = pairs[:, pl.ds(pl.multiple_of(x * owned, 128), owned)]
    kq = kq.astype(F32).astype(BF16)

    def phase(q, carry):
        @pl.when(q != me)
        def _():
            lat_copy(q, q, q).wait_recv()

        comp = lats[q].astype(F32).astype(BF16)
        turn = lax.dot_general(
            comp, kq, (((0,), (0,)), ((), ())), preferred_element_type=F32
        )
        turn = turn - jnp.round(turn * (1.0 / NK)) * NK
        cosine = quarter_sine(6.0 - jnp.abs(turn))
        folded = jnp.maximum(jnp.minimum(turn, 12.0 - turn), -12.0 - turn)
        sine = quarter_sine(folded)
        cb = cosine.astype(BF16)
        rows = pl.ds(pl.multiple_of(q * rloc, rloc), rloc)
        phase_a[rows, :owned] = cb
        phase_a[rows, owned:] = sine.astype(BF16)
        phase_b[rows, :owned] = (-sine).astype(BF16)
        phase_b[rows, owned:] = cb
        return carry

    lax.fori_loop(0, shards, phase, 0)

    def along_mom(step):
        dist = step + 1
        for c in range(chunks):
            for sign in (-1, 1):
                j = z + sign * dist

                @pl.when((j >= 0) & (j < moms))
                def _(j=j, c=c):
                    slot = j * lat_n + x
                    tab_copy(gath.at[c, slot], slot, c, 0).wait_recv()
                    pass_on(gath.at[c, slot], slot, c)

    loop(moms - 1, along_mom)

    def from_lat(c):
        for dist in range(1, lat_n):
            for sign in (-1, 1):
                i = x + sign * dist

                @pl.when((i >= 0) & (i < lat_n))
                def _(i=i):
                    def one(j):
                        slot = j * lat_n + i
                        tab_copy(gath.at[c, slot], slot, c, 2).wait_recv()
                        if lat_n > 2:
                            pass_on(gath.at[c, slot], slot, c, (2, 3))

                    loop(moms, one)

    lcopy.wait()
    group = math.gcd(shards, 8)
    kdim = group * rloc
    nblk = 4

    for c in range(chunks):
        own[c].wait()
        from_lat(c)

        def contract(g):
            pieces = [
                [gath[c, g * group + s, part].reshape(mc * nb_loc, rloc)
                 for s in range(group)]
                for part in (0, 1)
            ]
            rows = pl.ds(g * kdim, kdim)
            return jnp.dot(
                jnp.concatenate(pieces[0], 1), phase_a[rows, :],
                preferred_element_type=F32,
            ) + jnp.dot(
                jnp.concatenate(pieces[1], 1), phase_b[rows, :],
                preferred_element_type=F32,
            )

        bloch[...] = contract(0).reshape(bloch.shape)
        if shards > group:
            def add(g, carry):
                bloch[...] += contract(g).reshape(bloch.shape)
                return carry
            lax.fori_loop(1, shards // group, add, 0)

        def left_step(it, carry):
            eight = it // lane_tiles
            l0 = pl.multiple_of((it % lane_tiles) * 128, 128)
            lanes = pl.ds(l0, 128)
            lanes_im = pl.ds(l0 + owned, 128)
            for n0 in range(0, 8, nblk):
                tre = [None] * nblk
                tim = [None] * nblk
                for m in range(mc):
                    lre = lbuf[0, c * mc + m, :, lanes]
                    lim = lbuf[1, c * mc + m, :, lanes]
                    at = m * (nb_loc // 8) + eight
                    for n in range(nblk):
                        row = pl.ds(n0 + n, 1)
                        bre = jnp.broadcast_to(bloch[at, row, lanes], (bands, 128))
                        bim = jnp.broadcast_to(bloch[at, row, lanes_im], (bands, 128))
                        a = lre * bre + lim * bim
                        b = lre * bim - lim * bre
                        tre[n] = a if m == 0 else tre[n] + a
                        tim[n] = b if m == 0 else tim[n] + b
                for n in range(nblk):
                    col = eight * 8 + n0 + n
                    tr = tre[n].reshape(bands // 8, 8, 128)
                    ti = tim[n].reshape(bands // 8, 8, 128)
                    if c > 0:
                        tr = tr + tmine[0, col, :, :, lanes]
                        ti = ti + tmine[1, col, :, :, lanes]
                    tmine[0, col, :, :, lanes] = tr
                    tmine[1, col, :, :, lanes] = ti
            return carry

        lax.fori_loop(0, (nb_loc // 8) * lane_tiles, left_step, 0)

    tswap = pltpu.make_async_remote_copy(
        src_ref=tmine, dst_ref=tother,
        send_sem=swap_send.at[1], recv_sem=swap_recv.at[1],
        device_id={"band": other}, device_id_type=pl.DeviceIdType.MESH,
    )
    tswap.start()

    kblk = 8

    def right_half(tref, rref, row0, first):
        def body(it, carry):
            eight = it // lane_tiles
            k0 = eight * 8
            lanes = pl.ds(pl.multiple_of((it % lane_tiles) * 128, 128), 128)
            cre = [None] * kblk
            cim = [None] * kblk
            for n in range(nb_loc):
                vre = rref[0, n, pl.ds(row0, half), lanes]
                vim = rref[1, n, pl.ds(row0, half), lanes]
                for k in range(kblk):
                    row = pl.ds(k, 1)
                    tr = jnp.broadcast_to(tref[0, n, eight, row, lanes], (half, 128))
                    ti = jnp.broadcast_to(tref[1, n, eight, row, lanes], (half, 128))
                    a = tr * vre - ti * vim
                    b = tr * vim + ti * vre
                    cre[k] = a if n == 0 else cre[k] + a
                    cim[k] = b if n == 0 else cim[k] + b
            for k in range(kblk):
                if not first:
                    cre[k] = cre[k] + out[0, k0 + k, :, lanes]
                    cim[k] = cim[k] + out[1, k0 + k, :, lanes]
                out[0, k0 + k, :, lanes] = cre[k]
                out[1, k0 + k, :, lanes] = cim[k]
            return carry

        lax.fori_loop(0, (bands // kblk) * lane_tiles, body, 0)

    right_half(tmine, rbuf, pl.multiple_of(core * half, 8), True)
    rswap.wait_recv()
    tswap.wait_recv()
    right_half(tother, rother, 0, False)

    rswap.wait_send()
    tswap.wait_send()

    def lat_done(q, carry):
        @pl.when(q != me)
        def _():
            lat_copy(q, me, q).wait_send()
        return carry

    lax.fori_loop(0, shards, lat_done, 0)

    def tab_done(slot, carry):
        conds = sent_ways(slot)
        for c in range(chunks):
            for way in range(4):
                @pl.when(conds[way])
                def _(way=way, c=c):
                    tab_copy(gath.at[c, slot], slot, c, way).wait_send()
        return carry

    lax.fori_loop(0, shards, tab_done, 0)


def per_device(moms, lat_n, table, lattice, pairs, left_rot, right_rotation):
    tab = jnp.transpose(table, (1, 2, 3, 0))
    lat = jnp.transpose(lattice, (1, 0))
    lef = jnp.transpose(left_rot, (1, 2, 3, 0))
    rig = jnp.transpose(right_rotation, (1, 2, 3, 0))
    bands = tab.shape[1]
    nb_loc = tab.shape[2]
    rloc = tab.shape[3]
    owned = lef.shape[3]
    shards = moms * lat_n
    chunks = 4
    mc = bands // chunks
    cfg = (moms, lat_n, chunks, mc, nb_loc, owned, bands)
    anyspace = pl.BlockSpec(memory_space=pl.ANY)
    vmem = pl.BlockSpec(memory_space=pltpu.VMEM)
    dma = pltpu.SemaphoreType.DMA
    res = pl.pallas_call(
        functools.partial(kernel, cfg),
        out_shape=jax.ShapeDtypeStruct((2, bands, nb_loc, owned), F32),
        in_specs=[anyspace, anyspace, vmem, anyspace, anyspace],
        out_specs=vmem,
        scratch_shapes=[
            pltpu.VMEM((chunks, shards, 2, mc, nb_loc, rloc), BF16),
            pltpu.VMEM((shards, lat.shape[0], rloc), jnp.int32),
            pltpu.VMEM((shards * rloc, 2 * owned), BF16),
            pltpu.VMEM((shards * rloc, 2 * owned), BF16),
            pltpu.VMEM((mc * nb_loc // 8, 8, 2 * owned), F32),
            pltpu.VMEM(lef.shape, F32),
            pltpu.VMEM(rig.shape, F32),
            pltpu.VMEM((2, nb_loc, nb_loc, owned), F32),
            pltpu.VMEM((2, nb_loc, bands // 8, 8, owned), F32),
            pltpu.VMEM((2, nb_loc, bands // 8, 8, owned), F32),
            dma((shards,)),
            dma((shards,)),
            dma((4, shards, chunks)),
            dma((shards, chunks)),
            dma((chunks + 1,)),
            dma((2,)),
            dma((2,)),
            dma((2,)),
        ],
        compiler_params=pltpu.CompilerParams(
            collective_id=0, has_side_effects=True,
            vmem_limit_bytes=60 * 1024 * 1024,
        ),
    )(tab, lat, pairs, lef, rig)
    return jnp.transpose(res, (3, 0, 1, 2))


def solution(mesh):
    in_specs = (
        P(("groups", "mom", "lat"), None, None, "band"),
        P(("mom", "lat"), None),
        P(None, ("groups", "mom")),
        P(("groups", "mom", "lat"), None, None, None),
        P(("groups", "mom", "lat"), None, "band", None),
    )
    out_specs = P(("groups", "mom", "lat"), None, None, "band")
    body = functools.partial(per_device, mesh.shape["mom"], mesh.shape["lat"])
    return jax.shard_map(
        body, mesh=mesh, in_specs=in_specs, out_specs=out_specs, check_vma=False
    )
```

```python
import functools
import math

import jax
import jax.numpy as jnp
import numpy as np
from jax import lax
from jax.experimental import pallas as pl
from jax.experimental.pallas import tpu as pltpu
from jax.sharding import PartitionSpec as P

NK = 24
LAG = 1
F32 = jnp.float32
BF16 = jnp.bfloat16


def _sine_fit():
    b = 6.0 * np.sin(np.linspace(1e-3, math.pi / 2, 400))
    cols = np.stack([b ** (2 * j + 1) for j in range(5)], 1)
    scale = np.abs(cols).max(0)
    sol = np.linalg.lstsq(cols / scale, np.sin(math.pi * b / 12), rcond=None)[0]
    return [float(np.float32(v)) for v in sol / scale]


SINE = _sine_fit()


def quarter_sine(b):
    x = b * b
    acc = x * SINE[4] + SINE[3]
    acc = acc * x + SINE[2]
    acc = acc * x + SINE[1]
    acc = acc * x + SINE[0]
    return acc * b


def loop(count, body):
    if count <= 4:
        for i in range(count):
            body(i)
    else:
        def step(i, carry):
            body(i)
            return carry
        lax.fori_loop(0, count, step, 0)


def kernel(
    cfg, table, lattice, pairs, left, right, out,
    gath, lats, phase_a, phase_b, bloch, bother, mids, lbuf, rbuf, rother,
    send_sem, mom_recv, lat_recv, own_sem, in_sem, swap_send, swap_recv,
):
    moms, lat_n, chunks, mc, nb_loc, owned, bands = cfg
    shards = moms * lat_n
    z = lax.axis_index("mom")
    x = lax.axis_index("lat")
    core = lax.axis_index("band")
    me = z * lat_n + x
    other = 1 - core
    rloc = table.shape[3]
    lane_tiles = owned // 128

    lcopy = pltpu.make_async_copy(left, lbuf, in_sem.at[0])
    rcopy = pltpu.make_async_copy(right, rbuf, in_sem.at[1])
    lcopy.start()
    rcopy.start()

    barrier = pltpu.get_barrier_semaphore()

    near = (
        (z < moms - 1, {"mom": z + 1}),
        (z > 0, {"mom": z - 1}),
        (x < lat_n - 1, {"lat": x + 1}),
        (x > 0, {"lat": x - 1}),
    )
    for cond, dev in near:
        @pl.when(cond)
        def _(dev=dev):
            pl.semaphore_signal(
                barrier, inc=1, device_id=dev,
                device_id_type=pl.DeviceIdType.MESH,
            )
    pl.semaphore_signal(
        barrier, inc=1, device_id={"band": other},
        device_id_type=pl.DeviceIdType.MESH,
    )
    pl.semaphore_wait(barrier, 1 + sum(c.astype(jnp.int32) for c, _ in near))

    lat_item = chunks

    def place(slot, c):
        return lats.at[slot] if c == lat_item else gath.at[c, slot]

    def tab_copy(src, slot, c, way):
        if way < 2:
            recv = mom_recv.at[slot // lat_n, c]
        else:
            recv = lat_recv.at[slot if lat_n > 2 else 0, c]
        return pltpu.make_async_remote_copy(
            src_ref=src, dst_ref=place(slot, c),
            send_sem=send_sem.at[way, int(c == lat_item)], recv_sem=recv,
            device_id=near[way][1], device_id_type=pl.DeviceIdType.MESH,
        )

    def sent_ways(slot):
        j = slot // lat_n
        i = slot % lat_n
        return (
            (i == x) & (j <= z) & (z < moms - 1),
            (i == x) & (j >= z) & (z > 0),
            (i <= x) & (x < lat_n - 1),
            (i >= x) & (x > 0),
        )

    def pass_on(src, slot, c, ways=(0, 1, 2, 3)):
        conds = sent_ways(slot)
        for way in ways:
            @pl.when(conds[way])
            def _(way=way):
                tab_copy(src, slot, c, way).start()

    def start_own(c):
        src = lattice if c == lat_item else table.at[:, pl.ds(c * mc, mc)]
        pass_on(src, me, c)

    lat_own = pltpu.make_async_copy(lattice, lats.at[me], own_sem.at[chunks])
    lat_own.start()
    for c in (lat_item, 0, 1):
        start_own(c)
    own = [
        pltpu.make_async_copy(
            table.at[:, pl.ds(c * mc, mc)], gath.at[c, me], own_sem.at[c]
        )
        for c in range(chunks)
    ]
    for c in range(chunks):
        own[c].start()

    def tab_copy_all(ref, recv=None, send=None):
        return pltpu.make_async_remote_copy(
            src_ref=ref, dst_ref=ref,
            send_sem=send_sem.at[0, 0] if send is None else send,
            recv_sem=lat_recv.at[0, 0] if recv is None else recv,
            device_id={"band": other}, device_id_type=pl.DeviceIdType.MESH,
        )

    def along_mom(dist, c):
        for sign in (-1, 1):
            j = z + sign * dist

            @pl.when((j >= 0) & (j < moms))
            def _(j=j):
                slot = j * lat_n + x
                tab_copy(place(slot, c), slot, c, 0).wait_recv()
                pass_on(place(slot, c), slot, c)

    def from_lat(c):
        if lat_n == 2:
            every = lats if c == lat_item else gath.at[c]
            tab_copy_all(every.at[pl.ds(0, moms)], lat_recv.at[0, c]).wait_recv()
            return
        for dist in range(1, lat_n):
            for sign in (-1, 1):
                i = x + sign * dist

                @pl.when((i >= 0) & (i < lat_n))
                def _(i=i):
                    def one(j):
                        slot = j * lat_n + i
                        tab_copy(place(slot, c), slot, c, 2).wait_recv()
                        pass_on(place(slot, c), slot, c, (2, 3))

                    loop(moms, one)

    half = nb_loc
    rcopy.wait()
    rswap = pltpu.make_async_remote_copy(
        src_ref=rbuf.at[:, :, pl.ds(pl.multiple_of(other * half, 8), half)],
        dst_ref=rother, send_sem=swap_send.at[0], recv_sem=swap_recv.at[0],
        device_id={"band": other}, device_id_type=pl.DeviceIdType.MESH,
    )
    rswap.start()

    kq = pairs[:, pl.ds(pl.multiple_of(x * owned, 128), owned)]
    kq = kq.astype(F32).astype(BF16)

    def phase(q, carry):
        comp = lats[q].astype(F32).astype(BF16)
        turn = lax.dot_general(
            comp, kq, (((0,), (0,)), ((), ())), preferred_element_type=F32
        )
        turn = turn - jnp.round(turn * (1.0 / NK)) * NK
        cosine = quarter_sine(6.0 - jnp.abs(turn))
        folded = jnp.maximum(jnp.minimum(turn, 12.0 - turn), -12.0 - turn)
        sine = quarter_sine(folded)
        cb = cosine.astype(BF16)
        rows = pl.ds(pl.multiple_of(q * rloc, rloc), rloc)
        phase_a[rows, :owned] = cb
        phase_a[rows, owned:] = sine.astype(BF16)
        phase_b[rows, :owned] = (-sine).astype(BF16)
        phase_b[rows, owned:] = cb
        return carry


    group = math.gcd(shards, 8)
    kdim = group * rloc
    eights = nb_loc // 8

    def contract(c, g):
        pieces = [
            [gath[c, g * group + s, part].reshape(mc * nb_loc, rloc)
             for s in range(group)]
            for part in (0, 1)
        ]
        rows = pl.ds(g * kdim, kdim)
        return jnp.dot(
            jnp.concatenate(pieces[0], 1), phase_a[rows, :],
            preferred_element_type=F32,
        ) + jnp.dot(
            jnp.concatenate(pieces[1], 1), phase_b[rows, :],
            preferred_element_type=F32,
        )

    def band_swap(c):
        return pltpu.make_async_remote_copy(
            src_ref=bloch.at[c], dst_ref=bother.at[c],
            send_sem=swap_send.at[c + 1], recv_sem=swap_recv.at[c + 1],
            device_id={"band": other}, device_id_type=pl.DeviceIdType.MESH,
        )

    def right_part(bref, rref, row0, first):
        def body(lt, carry):
            l0 = pl.multiple_of(lt * 128, 128)
            lanes = pl.ds(l0, 128)
            lanes_im = pl.ds(l0 + owned, 128)
            for m0 in range(0, mc, mblk):
                cre = [None] * mblk
                cim = [None] * mblk
                for n in range(nb_loc):
                    vre = rref[0, n, pl.ds(row0, half), lanes]
                    vim = rref[1, n, pl.ds(row0, half), lanes]
                    for m in range(mblk):
                        at = (m0 + m) * eights + n // 8
                        row = pl.ds(n % 8, 1)
                        br = jnp.broadcast_to(bref[at, row, lanes], (half, 128))
                        bi = jnp.broadcast_to(bref[at, row, lanes_im], (half, 128))
                        a = br * vre - bi * vim
                        b = br * vim + bi * vre
                        cre[m] = a if n == 0 else cre[m] + a
                        cim[m] = b if n == 0 else cim[m] + b
                for m in range(mblk):
                    if not first:
                        cre[m] = cre[m] + mids[0, m0 + m, :, lanes]
                        cim[m] = cim[m] + mids[1, m0 + m, :, lanes]
                    mids[0, m0 + m, :, lanes] = cre[m]
                    mids[1, m0 + m, :, lanes] = cim[m]
            return carry

        lax.fori_loop(0, lane_tiles, body, 0)

    def left_part(c):
        def body(it, carry):
            eight = it // lane_tiles
            lanes = pl.ds(pl.multiple_of((it % lane_tiles) * 128, 128), 128)
            cre = [None] * 8
            cim = [None] * 8
            for m in range(mc):
                mre = mids[0, m, :, lanes]
                mim = mids[1, m, :, lanes]
                for k in range(8):
                    row = pl.ds(k, 1)
                    lr = jnp.broadcast_to(lbuf[0, c * mc + m, eight, row, lanes], (half, 128))
                    li = jnp.broadcast_to(lbuf[1, c * mc + m, eight, row, lanes], (half, 128))
                    a = lr * mre + li * mim
                    b = lr * mim - li * mre
                    cre[k] = a if m == 0 else cre[k] + a
                    cim[k] = b if m == 0 else cim[k] + b
            for k in range(8):
                at = eight * 8 + k
                if c > 0:
                    cre[k] = cre[k] + out[0, at, :, lanes]
                    cim[k] = cim[k] + out[1, at, :, lanes]
                out[0, at, :, lanes] = cre[k]
                out[1, at, :, lanes] = cim[k]
            return carry

        lax.fori_loop(0, (bands // 8) * lane_tiles, body, 0)

    mblk = min(mc, 8)

    def chunk(c):
        own[c].wait()
        from_lat(c)
        bloch[c] = contract(c, 0).reshape(bloch.shape[1:])
        if shards > group:
            def add(g, carry):
                bloch[c] += contract(c, g).reshape(bloch.shape[1:])
                return carry
            lax.fori_loop(1, shards // group, add, 0)
        band_swap(c).start()
        right_part(bloch.at[c], rbuf, pl.multiple_of(core * half, 8), True)
        if c == 0:
            rswap.wait_recv()
            lcopy.wait()
        band_swap(c).wait_recv()
        right_part(bother.at[c], rother, 0, False)
        left_part(c)

    for wave in range(1, chunks + moms + LAG):
        if wave < moms:
            along_mom(wave, lat_item)
        if 2 <= wave + 1 < chunks:
            start_own(wave + 1)
        for dist in range(1, moms):
            c = wave - dist
            if 0 <= c < chunks:
                along_mom(dist, c)
        if wave == moms:
            from_lat(lat_item)
            lat_own.wait()
            lax.fori_loop(0, shards, phase, 0)
        done = wave - moms - LAG
        if 0 <= done < chunks:
            chunk(done)

    for c in range(chunks):
        band_swap(c).wait_send()
    rswap.wait_send()

    def way_done(way, count, cond):
        @pl.when(cond)
        def _():
            tab_copy_all(
                gath.at[:, pl.ds(0, count)], send=send_sem.at[way, 0]
            ).wait_send()
            tab_copy_all(
                lats.at[pl.ds(0, count)], send=send_sem.at[way, 1]
            ).wait_send()

    for at in range(moms - 1):
        way_done(0, at + 1, z == at)
        way_done(1, at + 1, z == moms - 1 - at)
    for at in range(lat_n - 1):
        way_done(2, (at + 1) * moms, x == at)
        way_done(3, (at + 1) * moms, x == lat_n - 1 - at)


def per_device(moms, lat_n, table, lattice, pairs, left_rot, right_rotation):
    tab = jnp.transpose(table, (1, 2, 3, 0))
    lat = jnp.transpose(lattice, (1, 0))
    lef = jnp.transpose(left_rot, (1, 2, 3, 0))
    rig = jnp.transpose(right_rotation, (1, 2, 3, 0))
    bands = tab.shape[1]
    lef = lef.reshape(2, bands, bands // 8, 8, lef.shape[3])
    nb_loc = tab.shape[2]
    rloc = tab.shape[3]
    owned = rig.shape[3]
    shards = moms * lat_n
    chunks = 4
    mc = bands // chunks
    cfg = (moms, lat_n, chunks, mc, nb_loc, owned, bands)
    anyspace = pl.BlockSpec(memory_space=pl.ANY)
    vmem = pl.BlockSpec(memory_space=pltpu.VMEM)
    dma = pltpu.SemaphoreType.DMA
    res = pl.pallas_call(
        functools.partial(kernel, cfg),
        out_shape=pltpu.VMEM((2, bands, nb_loc, owned), F32),
        in_specs=[anyspace, anyspace, vmem, anyspace, anyspace],
        out_specs=vmem,
        scratch_shapes=[
            pltpu.VMEM((chunks, shards, 2, mc, nb_loc, rloc), BF16),
            pltpu.VMEM((shards, lat.shape[0], rloc), jnp.int32),
            pltpu.VMEM((shards * rloc, 2 * owned), BF16),
            pltpu.VMEM((shards * rloc, 2 * owned), BF16),
            pltpu.VMEM((chunks, mc * nb_loc // 8, 8, 2 * owned), F32),
            pltpu.VMEM((chunks, mc * nb_loc // 8, 8, 2 * owned), F32),
            pltpu.VMEM((2, mc, nb_loc, owned), F32),
            pltpu.VMEM(lef.shape, F32),
            pltpu.VMEM(rig.shape, F32),
            pltpu.VMEM((2, nb_loc, nb_loc, owned), F32),
            dma((4, 2)),
            dma((moms, chunks + 1)),
            dma((shards if lat_n > 2 else 1, chunks + 1)),
            dma((chunks + 1,)),
            dma((2,)),
            dma((chunks + 1,)),
            dma((chunks + 1,)),
        ],
        compiler_params=pltpu.CompilerParams(
            collective_id=0, has_side_effects=True,
            vmem_limit_bytes=60 * 1024 * 1024,
        ),
    )(tab, lat, pairs, lef, rig)
    return jnp.transpose(res, (3, 0, 1, 2))


def solution(mesh):
    in_specs = (
        P(("groups", "mom", "lat"), None, None, "band"),
        P(("mom", "lat"), None),
        P(None, ("groups", "mom")),
        P(("groups", "mom", "lat"), None, None, None),
        P(("groups", "mom", "lat"), None, "band", None),
    )
    out_specs = P(("groups", "mom", "lat"), None, None, "band")
    body = functools.partial(per_device, mesh.shape["mom"], mesh.shape["lat"])
    return jax.shard_map(
        body, mesh=mesh, in_specs=in_specs, out_specs=out_specs, check_vma=False
    )
```

```python
import functools
import math

import jax
import jax.numpy as jnp
import numpy as np
from jax import lax
from jax.experimental import pallas as pl
from jax.experimental.pallas import tpu as pltpu
from jax.sharding import PartitionSpec as P

NK = 24
LAG = 1
F32 = jnp.float32
BF16 = jnp.bfloat16


def _sine_fit():
    b = 6.0 * np.sin(np.linspace(1e-3, math.pi / 2, 400))
    cols = np.stack([b ** (2 * j + 1) for j in range(5)], 1)
    scale = np.abs(cols).max(0)
    sol = np.linalg.lstsq(cols / scale, np.sin(math.pi * b / 12), rcond=None)[0]
    return [float(np.float32(v)) for v in sol / scale]


SINE = _sine_fit()


def quarter_sine(b):
    x = b * b
    acc = x * SINE[4] + SINE[3]
    acc = acc * x + SINE[2]
    acc = acc * x + SINE[1]
    acc = acc * x + SINE[0]
    return acc * b


def loop(count, body):
    if count <= 4:
        for i in range(count):
            body(i)
    else:
        def step(i, carry):
            body(i)
            return carry
        lax.fori_loop(0, count, step, 0)


def kernel(
    cfg, table, lattice, pairs, left, right, out,
    gath, lats, phase_a, phase_b, bloch, bother, mids, lbuf, rbuf, rother,
    send_sem, mom_recv, lat_recv, own_sem, in_sem, swap_send, swap_recv,
):
    moms, lat_n, chunks, mc, nb_loc, owned, bands = cfg
    shards = moms * lat_n
    z = lax.axis_index("mom")
    x = lax.axis_index("lat")
    core = lax.axis_index("band")
    me = z * lat_n + x
    other = 1 - core
    rloc = table.shape[3]
    lane_tiles = owned // 128

    lcopy = pltpu.make_async_copy(left, lbuf, in_sem.at[0])
    rcopy = pltpu.make_async_copy(right, rbuf, in_sem.at[1])
    lcopy.start()
    rcopy.start()

    barrier = pltpu.get_barrier_semaphore()

    near = (
        (z < moms - 1, {"mom": z + 1}),
        (z > 0, {"mom": z - 1}),
        (x < lat_n - 1, {"lat": x + 1}),
        (x > 0, {"lat": x - 1}),
    )
    for cond, dev in near:
        @pl.when(cond)
        def _(dev=dev):
            pl.semaphore_signal(
                barrier, inc=1, device_id=dev,
                device_id_type=pl.DeviceIdType.MESH,
            )
    pl.semaphore_signal(
        barrier, inc=1, device_id={"band": other},
        device_id_type=pl.DeviceIdType.MESH,
    )
    pl.semaphore_wait(barrier, 1 + sum(c.astype(jnp.int32) for c, _ in near))

    lat_item = chunks

    def place(slot, c):
        return lats.at[slot] if c == lat_item else gath.at[c, slot]

    def tab_copy(src, slot, c, way):
        if way < 2:
            recv = mom_recv.at[slot // lat_n, c]
        else:
            recv = lat_recv.at[slot if lat_n > 2 else 0, c]
        return pltpu.make_async_remote_copy(
            src_ref=src, dst_ref=place(slot, c),
            send_sem=send_sem.at[way, int(c == lat_item)], recv_sem=recv,
            device_id=near[way][1], device_id_type=pl.DeviceIdType.MESH,
        )

    def sent_ways(slot):
        j = slot // lat_n
        i = slot % lat_n
        return (
            (i == x) & (j <= z) & (z < moms - 1),
            (i == x) & (j >= z) & (z > 0),
            (i <= x) & (x < lat_n - 1),
            (i >= x) & (x > 0),
        )

    def pass_on(src, slot, c, ways=(0, 1, 2, 3)):
        conds = sent_ways(slot)
        for way in ways:
            @pl.when(conds[way])
            def _(way=way):
                tab_copy(src, slot, c, way).start()

    def start_own(c):
        src = lattice if c == lat_item else table.at[:, pl.ds(c * mc, mc)]
        pass_on(src, me, c)

    lat_own = pltpu.make_async_copy(lattice, lats.at[me], own_sem.at[chunks])
    lat_own.start()
    for c in (lat_item, 0, 1):
        start_own(c)
    own = [
        pltpu.make_async_copy(
            table.at[:, pl.ds(c * mc, mc)], gath.at[c, me], own_sem.at[c]
        )
        for c in range(chunks)
    ]
    for c in range(chunks):
        own[c].start()

    def tab_copy_all(ref, recv=None, send=None):
        return pltpu.make_async_remote_copy(
            src_ref=ref, dst_ref=ref,
            send_sem=send_sem.at[0, 0] if send is None else send,
            recv_sem=lat_recv.at[0, 0] if recv is None else recv,
            device_id={"band": other}, device_id_type=pl.DeviceIdType.MESH,
        )

    def along_mom(dist, c):
        for sign in (-1, 1):
            j = z + sign * dist

            @pl.when((j >= 0) & (j < moms))
            def _(j=j):
                slot = j * lat_n + x
                tab_copy(place(slot, c), slot, c, 0).wait_recv()
                pass_on(place(slot, c), slot, c)

    def from_lat(c):
        if lat_n == 2:
            every = lats if c == lat_item else gath.at[c]
            tab_copy_all(every.at[pl.ds(0, moms)], lat_recv.at[0, c]).wait_recv()
            return
        for dist in range(1, lat_n):
            for sign in (-1, 1):
                i = x + sign * dist

                @pl.when((i >= 0) & (i < lat_n))
                def _(i=i):
                    def one(j):
                        slot = j * lat_n + i
                        tab_copy(place(slot, c), slot, c, 2).wait_recv()
                        pass_on(place(slot, c), slot, c, (2, 3))

                    loop(moms, one)

    half = nb_loc
    rcopy.wait()
    rswap = pltpu.make_async_remote_copy(
        src_ref=rbuf.at[:, :, pl.ds(pl.multiple_of(other * half, 8), half)],
        dst_ref=rother, send_sem=swap_send.at[0], recv_sem=swap_recv.at[0],
        device_id={"band": other}, device_id_type=pl.DeviceIdType.MESH,
    )
    rswap.start()

    kq = pairs[:, pl.ds(pl.multiple_of(x * owned, 128), owned)]
    kq = kq.astype(F32).astype(BF16)

    def phase(q, carry):
        comp = lats[q].astype(F32).astype(BF16)
        turn = lax.dot_general(
            comp, kq, (((0,), (0,)), ((), ())), preferred_element_type=F32
        )
        turn = turn - jnp.round(turn * (1.0 / NK)) * NK
        cosine = quarter_sine(6.0 - jnp.abs(turn))
        folded = jnp.maximum(jnp.minimum(turn, 12.0 - turn), -12.0 - turn)
        sine = quarter_sine(folded)
        cb = cosine.astype(BF16)
        rows = pl.ds(pl.multiple_of(q * rloc, rloc), rloc)
        phase_a[rows, :owned] = cb
        phase_a[rows, owned:] = sine.astype(BF16)
        phase_b[rows, :owned] = (-sine).astype(BF16)
        phase_b[rows, owned:] = cb
        return carry


    group = math.gcd(shards, 8)
    kdim = group * rloc
    eights = nb_loc // 8

    def contract(c, g):
        pieces = [
            [gath[c, g * group + s, part].reshape(mc * nb_loc, rloc)
             for s in range(group)]
            for part in (0, 1)
        ]
        rows = pl.ds(g * kdim, kdim)
        return jnp.dot(
            jnp.concatenate(pieces[0], 1), phase_a[rows, :],
            preferred_element_type=F32,
        ) + jnp.dot(
            jnp.concatenate(pieces[1], 1), phase_b[rows, :],
            preferred_element_type=F32,
        )

    def band_swap(c):
        return pltpu.make_async_remote_copy(
            src_ref=bloch.at[c], dst_ref=bother.at[c],
            send_sem=swap_send.at[c + 1], recv_sem=swap_recv.at[c + 1],
            device_id={"band": other}, device_id_type=pl.DeviceIdType.MESH,
        )

    def right_part(bref, rref, row0, first, buf):
        def body(lt, carry):
            l0 = pl.multiple_of(lt * 128, 128)
            lanes = pl.ds(l0, 128)
            lanes_im = pl.ds(l0 + owned, 128)
            for m0 in range(0, mc, mblk):
                cre = [None] * mblk
                cim = [None] * mblk
                for n in range(nb_loc):
                    vre = rref[0, n, pl.ds(row0, half), lanes]
                    vim = rref[1, n, pl.ds(row0, half), lanes]
                    for m in range(mblk):
                        at = (m0 + m) * eights + n // 8
                        row = pl.ds(n % 8, 1)
                        br = jnp.broadcast_to(bref[at, row, lanes], (half, 128))
                        bi = jnp.broadcast_to(bref[at, row, lanes_im], (half, 128))
                        a = br * vre - bi * vim
                        b = br * vim + bi * vre
                        cre[m] = a if n == 0 else cre[m] + a
                        cim[m] = b if n == 0 else cim[m] + b
                for m in range(mblk):
                    if not first:
                        cre[m] = cre[m] + mids[buf, 0, m0 + m, :, lanes]
                        cim[m] = cim[m] + mids[buf, 1, m0 + m, :, lanes]
                    mids[buf, 0, m0 + m, :, lanes] = cre[m]
                    mids[buf, 1, m0 + m, :, lanes] = cim[m]
            return carry

        lax.fori_loop(0, lane_tiles, body, 0)

    def left_part(c):
        buf = c % 2

        def body(it, carry):
            eight = it // lane_tiles
            lanes = pl.ds(pl.multiple_of((it % lane_tiles) * 128, 128), 128)
            cre = [None] * 8
            cim = [None] * 8
            for m in range(mc):
                mre = mids[buf, 0, m, :, lanes]
                mim = mids[buf, 1, m, :, lanes]
                for k in range(8):
                    row = pl.ds(k, 1)
                    lr = jnp.broadcast_to(lbuf[0, c * mc + m, eight, row, lanes], (half, 128))
                    li = jnp.broadcast_to(lbuf[1, c * mc + m, eight, row, lanes], (half, 128))
                    a = lr * mre + li * mim
                    b = lr * mim - li * mre
                    cre[k] = a if m == 0 else cre[k] + a
                    cim[k] = b if m == 0 else cim[k] + b
            for k in range(8):
                at = eight * 8 + k
                if c > 0:
                    cre[k] = cre[k] + out[0, at, :, lanes]
                    cim[k] = cim[k] + out[1, at, :, lanes]
                out[0, at, :, lanes] = cre[k]
                out[1, at, :, lanes] = cim[k]
            return carry

        lax.fori_loop(0, (bands // 8) * lane_tiles, body, 0)

    mblk = min(mc, 8)

    def chunk(c):
        own[c].wait()
        from_lat(c)
        bloch[c] = contract(c, 0).reshape(bloch.shape[1:])
        if shards > group:
            def add(g, carry):
                bloch[c] += contract(c, g).reshape(bloch.shape[1:])
                return carry
            lax.fori_loop(1, shards // group, add, 0)
        band_swap(c).start()
        right_part(
            bloch.at[c], rbuf, pl.multiple_of(core * half, 8), True, c % 2
        )
        if c > 0:
            finish(c - 1)

    def finish(c):
        if c == 0:
            rswap.wait_recv()
            lcopy.wait()
        band_swap(c).wait_recv()
        right_part(bother.at[c], rother, 0, False, c % 2)
        left_part(c)

    for wave in range(1, chunks + moms + LAG):
        if wave < moms:
            along_mom(wave, lat_item)
        if 2 <= wave + 1 < chunks:
            start_own(wave + 1)
        for dist in range(1, moms):
            c = wave - dist
            if 0 <= c < chunks:
                along_mom(dist, c)
        if wave == moms:
            from_lat(lat_item)
            lat_own.wait()
            lax.fori_loop(0, shards, phase, 0)
        done = wave - moms - LAG
        if 0 <= done < chunks:
            chunk(done)
    finish(chunks - 1)

    for c in range(chunks):
        band_swap(c).wait_send()
    rswap.wait_send()

    def way_done(way, count, cond):
        @pl.when(cond)
        def _():
            tab_copy_all(
                gath.at[:, pl.ds(0, count)], send=send_sem.at[way, 0]
            ).wait_send()
            tab_copy_all(
                lats.at[pl.ds(0, count)], send=send_sem.at[way, 1]
            ).wait_send()

    for at in range(moms - 1):
        way_done(0, at + 1, z == at)
        way_done(1, at + 1, z == moms - 1 - at)
    for at in range(lat_n - 1):
        way_done(2, (at + 1) * moms, x == at)
        way_done(3, (at + 1) * moms, x == lat_n - 1 - at)


def per_device(moms, lat_n, table, lattice, pairs, left_rot, right_rotation):
    tab = jnp.transpose(table, (1, 2, 3, 0))
    lat = jnp.transpose(lattice, (1, 0))
    lef = jnp.transpose(left_rot, (1, 2, 3, 0))
    rig = jnp.transpose(right_rotation, (1, 2, 3, 0))
    bands = tab.shape[1]
    lef = lef.reshape(2, bands, bands // 8, 8, lef.shape[3])
    nb_loc = tab.shape[2]
    rloc = tab.shape[3]
    owned = rig.shape[3]
    shards = moms * lat_n
    chunks = 4
    mc = bands // chunks
    cfg = (moms, lat_n, chunks, mc, nb_loc, owned, bands)
    anyspace = pl.BlockSpec(memory_space=pl.ANY)
    vmem = pl.BlockSpec(memory_space=pltpu.VMEM)
    dma = pltpu.SemaphoreType.DMA
    res = pl.pallas_call(
        functools.partial(kernel, cfg),
        out_shape=pltpu.VMEM((2, bands, nb_loc, owned), F32),
        in_specs=[anyspace, anyspace, vmem, anyspace, anyspace],
        out_specs=vmem,
        scratch_shapes=[
            pltpu.VMEM((chunks, shards, 2, mc, nb_loc, rloc), BF16),
            pltpu.VMEM((shards, lat.shape[0], rloc), jnp.int32),
            pltpu.VMEM((shards * rloc, 2 * owned), BF16),
            pltpu.VMEM((shards * rloc, 2 * owned), BF16),
            pltpu.VMEM((chunks, mc * nb_loc // 8, 8, 2 * owned), F32),
            pltpu.VMEM((chunks, mc * nb_loc // 8, 8, 2 * owned), F32),
            pltpu.VMEM((2, 2, mc, nb_loc, owned), F32),
            pltpu.VMEM(lef.shape, F32),
            pltpu.VMEM(rig.shape, F32),
            pltpu.VMEM((2, nb_loc, nb_loc, owned), F32),
            dma((4, 2)),
            dma((moms, chunks + 1)),
            dma((shards if lat_n > 2 else 1, chunks + 1)),
            dma((chunks + 1,)),
            dma((2,)),
            dma((chunks + 1,)),
            dma((chunks + 1,)),
        ],
        compiler_params=pltpu.CompilerParams(
            collective_id=0, has_side_effects=True,
            vmem_limit_bytes=60 * 1024 * 1024,
        ),
    )(tab, lat, pairs, lef, rig)
    return jnp.transpose(res, (3, 0, 1, 2))


def solution(mesh):
    in_specs = (
        P(("groups", "mom", "lat"), None, None, "band"),
        P(("mom", "lat"), None),
        P(None, ("groups", "mom")),
        P(("groups", "mom", "lat"), None, None, None),
        P(("groups", "mom", "lat"), None, "band", None),
    )
    out_specs = P(("groups", "mom", "lat"), None, None, "band")
    body = functools.partial(per_device, mesh.shape["mom"], mesh.shape["lat"])
    return jax.shard_map(
        body, mesh=mesh, in_specs=in_specs, out_specs=out_specs, check_vma=False
    )
```
